32 devices in a mesh: section: 2 (over core), fsdp: 4 (over y, x), replica: 4 (over z).
Axes of the slice: x: 2, y: 2, z: 4, core: 2. Of those that a mesh axis runs over, the one named last changes fastest.
Arguments:
- images: bfloat16 [32, 197, 1024], P(('fsdp', 'replica')), may hold values from -6 to 6
- assign: int32 [16, 2], P(('fsdp', 'replica')), may hold values from 0 to 1, each once within a row
- cotangent: bfloat16 [32, 197, 1024], P(('fsdp', 'replica')), may hold values from -6 to 6
- norm_gain: bfloat16 [2, 2, 1024], P('section', None, 'fsdp'), may hold values from 0.25 to 1.75
- norm_shift: bfloat16 [2, 2, 1024], P('section', None, 'fsdp'), may hold values from -2.5 to 2.5
- input_weight: bfloat16 [2, 1024, 3072], P('section', 'fsdp'), may hold values from -0.1875 to 0.1875
- input_bias: bfloat16 [2, 2048], P('section', 'fsdp'), may hold values from -4 to 4
- output_weight: bfloat16 [2, 1024, 1024], P('section', 'fsdp'), may hold values from -1.5 to 1.5
- output_bias: bfloat16 [2, 1024], P('section', 'fsdp'), may hold values from -4 to 4
- upward_weight: bfloat16 [2, 1024, 4096], P('section', 'fsdp'), may hold values from -0.1875 to 0.1875
- upward_bias: bfloat16 [2, 4096], P('section', 'fsdp'), may hold values from -4 to 4
- down_weight: bfloat16 [2, 4096, 1024], P('section', 'fsdp'), may hold values from -0.09375 to 0.09375
- down_bias: bfloat16 [2, 1024], P('section', 'fsdp'), may hold values from -4 to 4
Outputs:
- ends: float32 [2, 32, 197, 1024], P('section', ('fsdp', 'replica'))
- grad_norm_gain: float32 [2, 2, 1024], P('section', None, 'fsdp')
- grad_norm_shift: float32 [2, 2, 1024], P('section', None, 'fsdp')
- grad_input_weight: float32 [2, 1024, 3072], P('section', 'fsdp')
- grad_input_bias: float32 [2, 2048], P('section', 'fsdp')
- grad_output_weight: float32 [2, 1024, 1024], P('section', 'fsdp')
- grad_output_bias: float32 [2, 1024], P('section', 'fsdp')
- grad_upward_weight: float32 [2, 1024, 4096], P('section', 'fsdp')
- grad_upward_bias: float32 [2, 4096], P('section', 'fsdp')
- grad_down_weight: float32 [2, 4096, 1024], P('section', 'fsdp')
- grad_down_bias: float32 [2, 1024], P('section', 'fsdp')
The draws below stay inside these ranges and needn't reach their ends.
Inputs may be any that keep to these rules, and one draw needn't show every extreme that they name: `assign`: each row is a permutation of the images of one device group; position m of a row is micro-batch m.
All inputs are finite; a program needn't handle non-finite values.
Results may differ from the reference program's by a relative error of at most 0.017.
Values may be sent and summed in bfloat16 or wider, within the bound.
No kernel may reach another device: no remote copies, remote signals or barrier semaphores. Data moves between devices by JAX's collectives and lax.ppermute only.
A program may use at most 256 MiB of HBM per device.

```python
import jax
import jax.numpy as jnp
from jax import lax

D = 1024
HEADS = 16
HD = 64
FF = 4096
SEQ = 197
IMG_DEV = 2
GROUPS = 16
IMAGES = 32


def shard_levels(rng, dims, split, smallest, largest):
    level, own = 1.0, jax.random.fold_in(rng, 6)
    for axis_at, blocks in split:
        heights = jnp.exp(jax.random.uniform(jax.random.fold_in(own, axis_at), (blocks,), jnp.float32, smallest / len(split), largest / len(split)))
        level = level * jnp.repeat(heights, dims[axis_at] // blocks).reshape([-1 if axis == axis_at else 1 for axis in range(len(dims))])
    return level


def gaussian(stream_key, shape, scale, most, cuts=(), held_as=jnp.bfloat16):
    drawn = scale * jax.random.normal(stream_key, shape, jnp.float32)
    if cuts:
        drawn = drawn * shard_levels(stream_key, shape, cuts, -0.22, 0.18)
    return jnp.clip(drawn, -most, most).astype(held_as)


def setup_inputs(seed: int = 0) -> dict:
    streams_of = jax.random.split(jax.random.key(seed), 14)
    return {
        "images": gaussian(streams_of[0], (IMAGES, SEQ, D), 1.0, 6.0, ((0, 16),)),
        "assign": jax.vmap(lambda own: jax.random.permutation(own, IMG_DEV))(jax.random.split(streams_of[1], GROUPS)).reshape((GROUPS, IMG_DEV)).astype(jnp.int32),
        "cotangent": gaussian(streams_of[2], (IMAGES, SEQ, D), 1.0, 6.0, ((0, 16),)),
        "norm_gain": jnp.clip(1.0 + 0.15 * jax.random.normal(streams_of[3], (2, 2, D), jnp.float32), 0.25, 1.75).astype(jnp.bfloat16),
        "norm_shift": gaussian(streams_of[4], (2, 2, D), 0.3, 2.5, ((0, 2), (2, 4))),
        "input_weight": gaussian(streams_of[5], (2, D, 3 * D), D ** -0.5, 0.1875, ((0, 2), (1, 4))),
        "input_bias": gaussian(streams_of[6], (2, 2 * D), 0.5, 4.0, ((0, 2), (1, 4))),
        "output_weight": gaussian(streams_of[7], (2, D, D), (D // 64) ** -0.5, 1.5, ((0, 2), (1, 4))),
        "output_bias": gaussian(streams_of[8], (2, D), 0.8, 4.0, ((0, 2), (1, 4))),
        "upward_weight": gaussian(streams_of[9], (2, D, FF), D ** -0.5, 0.1875, ((0, 2), (1, 4))),
        "upward_bias": gaussian(streams_of[10], (2, FF), 0.5, 4.0, ((0, 2), (1, 4))),
        "down_weight": gaussian(streams_of[11], (2, FF, D), FF ** -0.5, 0.09375, ((0, 2), (1, 4))),
        "down_bias": gaussian(streams_of[12], (2, D), 0.8, 4.0, ((0, 2), (1, 4))),
    }


@jax.custom_vjp
def low(v):
    return lax.optimization_barrier(v.astype(jnp.bfloat16)).astype(jnp.float32)

@jax.custom_vjp
def low_back(v):
    return v

def low_keep(v):
    return (low(v), None)

def low_pass(kept, grad):
    return (grad,)

def back_keep(v):
    return (v, None)

def back_low(kept, grad):
    return (low(grad),)
low.defvjp(low_keep, low_pass)
low_back.defvjp(back_keep, back_low)
EPS = 1e-06

def layer_norm(values, gain_row, shift_row):
    centred = values - lax.optimization_barrier(jnp.mean(values, axis=-1, keepdims=True))
    scaled = centred * lax.rsqrt(lax.optimization_barrier(jnp.mean(centred * centred, axis=-1, keepdims=True)) + EPS)
    return scaled * gain_row + shift_row

def product(left, right):
    return jnp.einsum('bsd,de->bse', left, right, precision=lax.Precision.HIGHEST)

def one_layer(inputs, params, index):
    norm_gain, norm_shift, input_weight, input_bias, output_weight, output_bias, upward_weight, upward_bias, down_weight, down_bias = params
    batch = inputs.shape[0]
    normed_one = low(layer_norm(inputs, norm_gain[index, 0], norm_shift[index, 0]))
    joint = product(normed_one, low(input_weight[index]))
    query_rows = low(low_back(joint[..., :D] + input_bias[index, :D]))
    key_rows = low(low_back(joint[..., D:2 * D]))
    value_rows = low(low_back(joint[..., 2 * D:] + input_bias[index, D:]))
    query_heads = query_rows.reshape(batch, SEQ, HEADS, HD)
    key_heads = key_rows.reshape(batch, SEQ, HEADS, HD)
    value_heads = value_rows.reshape(batch, SEQ, HEADS, HD)
    scores = low_back(jnp.einsum('bqhe,bkhe->bhqk', query_heads, key_heads, precision=lax.Precision.HIGHEST) * HD ** (-0.5))
    probs = low(jax.nn.softmax(scores, axis=-1))
    mixed = jnp.einsum('bhqk,bkhe->bqhe', probs, value_heads, precision=lax.Precision.HIGHEST).reshape(batch, SEQ, D)
    mixed = low(low_back(mixed))
    hidden = inputs + low_back(product(mixed, low(output_weight[index])) + output_bias[index])
    normed_two = low(layer_norm(hidden, norm_gain[index, 1], norm_shift[index, 1]))
    pre_active = low_back(product(normed_two, low(upward_weight[index])) + upward_bias[index])
    activated = low(jax.nn.gelu(pre_active, approximate=False))
    return hidden + low_back(product(activated, low(down_weight[index])) + down_bias[index])

def two_layers(inputs, params):
    middle = one_layer(inputs, params, 0)
    middle = low(low_back(middle))
    return one_layer(middle, params, 1)

def reference(images, assign, cotangent, norm_gain, norm_shift, input_weight, input_bias, output_weight, output_bias, upward_weight, upward_bias, down_weight, down_bias):
    groups = assign.shape[0]
    per_group = assign.shape[1]
    order = (jnp.arange(groups, dtype=jnp.int32)[:, None] * per_group + assign).reshape(-1).astype(jnp.int32)
    params = tuple((item.astype(jnp.float32) for item in (norm_gain, norm_shift, input_weight, input_bias, output_weight, output_bias, upward_weight, upward_bias, down_weight, down_bias)))
    ordered = images[order].reshape(groups, per_group, SEQ, D)
    seeds = cotangent.reshape(groups, per_group, SEQ, D)
    zero_grads = tuple((jnp.zeros_like(item) for item in params))

    def visit(totals, block):
        input_block, seed_block = block
        outputs, pull = jax.vjp(two_layers, input_block.astype(jnp.float32), params)
        grad_inputs, grad_params = pull(seed_block.astype(jnp.float32))
        totals = tuple((total + grad for total, grad in zip(totals, grad_params)))
        return (totals, (outputs, grad_inputs))
    totals, (finals, grads_in) = lax.scan(visit, zero_grads, (ordered, seeds))
    final_rows = finals.reshape(-1, SEQ, D)
    grad_rows = jnp.zeros(images.shape, jnp.float32).at[order].set(grads_in.reshape(-1, SEQ, D))
    ends = jnp.stack([grad_rows, final_rows])
    return (ends, totals[0], totals[1], totals[2], totals[3], totals[4], totals[5], totals[6], totals[7], totals[8], totals[9])
```

```python
import jax
import jax.numpy as jnp
from jax import lax
from jax.experimental import pallas as pl
from jax.experimental.pallas import tpu as pltpu
from jax.sharding import PartitionSpec as P

HD = 64
EPS = 1e-06
F32 = jnp.float32
BF16 = jnp.bfloat16


def dot(a, b, dims):
    return lax.dot_general(a, b, (dims, ((), ())), preferred_element_type=F32)


def nn(a, b):
    return dot(a, b, ((1,), (0,)))


def nt(a, b):
    return dot(a, b, ((1,), (1,)))


def tn(a, b):
    return dot(a, b, ((0,), (0,)))


def copy_block(index_ref, source_ref, target_ref):
    target_ref[...] = source_ref[...]


def permute_columns(values, index, width, inverse=False):
    rows, columns = values.shape
    count = columns // width
    if width % 128:
        blocks = values.reshape(rows, count, width)
        order = jnp.argsort(index) if inverse else index
        return jnp.take(blocks, order, axis=1).reshape(rows, columns)
    moved = pl.BlockSpec((rows, width), lambda i, at: (0, at[i]))
    kept = pl.BlockSpec((rows, width), lambda i, at: (0, i))
    return pl.pallas_call(
        copy_block,
        out_shape=jax.ShapeDtypeStruct(values.shape, values.dtype),
        grid_spec=pltpu.PrefetchScalarGridSpec(
            num_scalar_prefetch=1,
            grid=(count,),
            in_specs=[kept if inverse else moved],
            out_specs=moved if inverse else kept,
        ),
    )(index, values)


def normalize(values):
    centred = values - jnp.mean(values, axis=-1, keepdims=True)
    inverse = lax.rsqrt(jnp.mean(centred * centred, axis=-1, keepdims=True) + EPS)
    return centred * inverse, inverse


def norm_back(grad_normed, scaled, inverse, gain_row):
    grad_scaled = grad_normed * gain_row
    return inverse * (
        grad_scaled
        - jnp.mean(grad_scaled, axis=-1, keepdims=True)
        - scaled * jnp.mean(grad_scaled * scaled, axis=-1, keepdims=True)
    )


def gelu_pair(values):
    cdf = 0.5 * (1.0 + lax.erf(values * (0.5**0.5)))
    return values * cdf, cdf


class Links:
    def __init__(self, cores, fsdp, replica):
        self.cores, self.fsdp, self.replica = cores, fsdp, replica
        self.bits = fsdp.bit_length() - 1
        self.core = lax.axis_index("section")
        self.at = lax.axis_index("fsdp")
        self.row = lax.axis_index("replica")
        ascending = list(range(self.bits))
        self.order = (ascending, ascending[::-1])

    def swap(self, value):
        return lax.ppermute(value, "section", [(0, 1), (1, 0)])

    def step(self, value, k):
        pairs = [
            (s * self.fsdp + f, s * self.fsdp + (f ^ (1 << self.order[s][k])))
            for s in range(2)
            for f in range(self.fsdp)
        ]
        return lax.ppermute(value, ("section", "fsdp"), pairs)

    def offset(self, half, j):
        return sum(1 << self.order[half][k] for k in range(self.bits) if j >> k & 1)

    def block(self, half, j):
        return self.at ^ jnp.where(half == 0, self.offset(0, j), self.offset(1, j))

    def gather(self, own):
        pieces = [own]
        for k in range(self.bits):
            pieces += [self.step(piece, k) for piece in pieces]
        return pieces

    def line_sum(self, part):
        size, row = self.replica, self.row
        if size == 1:
            return part
        half = size // 2
        total = part
        for k in range(half - 1):
            moved = lax.ppermute(total, "replica", [(k, k + 1), (size - 1 - k, size - 2 - k)])
            total = (total.astype(F32) + moved.astype(F32)).astype(BF16)
        moved = lax.ppermute(total, "replica", [(half - 1, half), (half, half - 1)])
        total = (total.astype(F32) + moved.astype(F32)).astype(BF16)
        for k in reversed(range(half - 1)):
            moved = lax.ppermute(total, "replica", [(k + 1, k), (size - 2 - k, size - 1 - k)])
            total = jnp.where((row == k) | (row == size - 1 - k), moved, total)
        return total


def forward_layer(inputs, weights, small, order):
    in_out, upward, downward = weights
    gain, shift, in_bias, out_bias, up_bias, down_bias = small
    narrow, wide = order
    width = inputs.shape[1]
    rows = inputs.shape[0]
    heads = width // HD
    scaled_one, inverse_one = normalize(inputs)
    normed_one = permute_columns((scaled_one * gain[0] + shift[0]).astype(BF16), narrow, width // narrow.shape[0])
    joint = nn(normed_one, in_out[:, : 3 * width])
    query = (joint[:, :width] + in_bias[:width]).astype(BF16)
    key = joint[:, width : 2 * width].astype(BF16)
    value = (joint[:, 2 * width :] + in_bias[width:]).astype(BF16)
    split = lambda v: v.reshape(rows, heads, HD)
    scores = jnp.einsum("qhe,khe->hqk", split(query), split(key), preferred_element_type=F32) * HD ** (-0.5)
    top = jnp.max(scores, axis=-1, keepdims=True)
    log_total = top + jnp.log(jnp.sum(jnp.exp(scores - top), axis=-1, keepdims=True))
    probs = jnp.exp(scores - log_total).astype(BF16)
    mixed = jnp.einsum("hqk,khe->qhe", probs, split(value), preferred_element_type=F32)
    mixed = permute_columns(mixed.reshape(rows, width).astype(BF16), narrow, width // narrow.shape[0])
    hidden = inputs + nn(mixed, in_out[:, 3 * width :]) + out_bias
    scaled_two, inverse_two = normalize(hidden)
    normed_two = permute_columns((scaled_two * gain[1] + shift[1]).astype(BF16), narrow, width // narrow.shape[0])
    pre_active = nn(normed_two, upward) + up_bias
    active, cdf = gelu_pair(pre_active)
    wide_width = pre_active.shape[1]
    active = permute_columns(active.astype(BF16), wide, wide_width // wide.shape[0])
    result = hidden + nn(active, downward) + down_bias
    kept = (
        scaled_one, inverse_one, normed_one, query, key, value, log_total, mixed,
        scaled_two, inverse_two, normed_two, pre_active, active,
    )
    return result, kept


def solution(mesh):
    cores, fsdp, replica = (mesh.shape[name] for name in ("section", "fsdp", "replica"))

    def per_device(
        images, assign, cotangent, norm_gain, norm_shift, input_weight, input_bias,
        output_weight, output_bias, upward_weight, upward_bias, down_weight, down_bias,
    ):
        links = Links(cores, fsdp, replica)
        core, swap = links.core, links.swap
        first = core == 0
        width = images.shape[2]
        part = width // fsdp
        wide = down_weight.shape[1] * fsdp
        tall = down_weight.shape[1]
        half, tall_half = part // 2, tall // 2

        own_small = jnp.concatenate(
            [item.reshape(-1) for item in (norm_gain, norm_shift, input_bias, output_bias, upward_bias, down_bias)]
        )
        small_size = own_small.shape[0]
        own = (
            jnp.concatenate([input_weight[0], output_weight[0]], axis=1),
            upward_weight[0],
            down_weight[0],
        )
        padded = jnp.pad(own_small, (0, -small_size % 1024)).reshape(-1, 1024)
        small_rows = padded.shape[0]
        padded_other = swap(padded)
        other = tuple(swap(item) for item in own)
        smalls = jnp.concatenate(
            [jnp.where(first, padded, padded_other), jnp.where(first, padded_other, padded)], axis=0
        )
        small_pieces = jnp.stack(links.gather(smalls))
        small_order = jnp.stack([links.at ^ jnp.where(first, links.offset(0, j), links.offset(1, j)) for j in range(fsdp)])
        inverse_order = jnp.stack([
            jnp.where(first, *[jnp.sum(jnp.stack([
                jnp.where((links.at ^ links.offset(h, j)) == b, j, 0) for j in range(fsdp)])) for h in range(2)])
            for b in range(fsdp)
        ])
        small_all = jnp.take(small_pieces, inverse_order, axis=0)

        def small_of(layer):
            flat = small_all[:, layer * small_rows : (layer + 1) * small_rows].reshape(fsdp, -1)[:, :small_size]
            at, out = 0, []
            for count, lead in ((2 * part, 2), (2 * part, 2), (2 * part, 1), (part, 1), (4 * part, 1), (part, 1)):
                item = flat[:, at : at + count].astype(F32)
                at += count
                if lead == 2:
                    item = item.reshape(fsdp, 2, -1).transpose(1, 0, 2).reshape(2, -1)
                else:
                    item = item.reshape(-1)
                out.append(item)
            return out

        halves = (half, half, tall_half)

        def weights_of(layer):
            out = []
            for mine, theirs, size in zip(own, other, halves):
                shard = jnp.where(first == (layer == 0), mine, theirs)
                start = lax.dynamic_slice_in_dim(shard, core * size, size, 0)
                rest = lax.dynamic_slice_in_dim(shard, (1 - core) * size, size, 0)
                pieces = links.gather(start)
                swapped = [rest] + [swap(piece) for piece in pieces[1:]]
                out.append(jnp.concatenate(pieces + swapped, axis=0))
            return out

        def order_of():
            return jnp.stack(
                [2 * links.block(h, j) + h for h in (core, 1 - core) for j in range(fsdp)]
            ).astype(jnp.int32)

        index = order_of()
        order = (index, index)
        image_at = jnp.where(first, assign[0, 0], assign[0, 1])
        source = lax.dynamic_index_in_dim(images, image_at, 0, keepdims=False).astype(F32)
        seed = lax.dynamic_index_in_dim(cotangent, core, 0, keepdims=False)

        small = [small_of(layer) for layer in range(2)]
        weights = [weights_of(layer) for layer in range(2)]
        middle, kept_zero = forward_layer(source, weights[0], small[0], order)
        final, kept_one = forward_layer(middle.astype(BF16).astype(F32), weights[1], small[1], order)
        kept = [kept_zero, kept_one]

        def reduce_parts(make, size):
            sent = swap(make(1, 0, fsdp).astype(BF16))
            arrived = [(0, sent)]
            for k in reversed(range(links.bits)):
                low, high = 1 << k, 2 << k
                total = make(0, low, high)
                for base, item in arrived:
                    total = total + item[(low - base) * size : (high - base) * size].astype(F32)
                arrived.append((0, links.step(total.astype(BF16), k)))
            total = make(0, 0, 1)
            for base, item in arrived:
                total = total + item[:size].astype(F32)
            return links.line_sum(total.astype(BF16))

        def columns(values, h, low, high, size):
            start = (h * fsdp + low) * size
            return values[:, start : start + (high - low) * size]

        def backward_layer(grad_out, layer):
            in_out, upward, downward = weights[layer]
            gain = small[layer][0]
            (
                scaled_one, inverse_one, normed_one, query, key, value, log_total, mixed,
                scaled_two, inverse_two, normed_two, pre_active, active,
            ) = kept[layer]
            rows = grad_out.shape[0]
            heads = width // HD
            branch = grad_out.astype(BF16)
            g_down_bias = jnp.sum(branch.astype(F32), axis=0)
            g_down = reduce_parts(
                lambda h, low, high: tn(columns(active, h, low, high, tall_half), branch), tall_half
            )
            grad_active = permute_columns(nt(branch, downward), index, tall_half, inverse=True)
            cdf = 0.5 * (1.0 + lax.erf(pre_active * (0.5**0.5)))
            slope = cdf + pre_active * jnp.exp(-0.5 * pre_active * pre_active) * (0.5 / jnp.pi) ** 0.5
            grad_pre = (grad_active * slope).astype(BF16)
            g_up_bias = jnp.sum(grad_pre.astype(F32), axis=0)
            g_up = reduce_parts(
                lambda h, low, high: tn(columns(normed_two, h, low, high, half), grad_pre), half
            )
            grad_normed_two = permute_columns(nt(grad_pre, upward), index, half, inverse=True)
            gain_two = jnp.sum(grad_normed_two * scaled_two, axis=0)
            shift_two = jnp.sum(grad_normed_two, axis=0)
            grad_hidden = grad_out + norm_back(grad_normed_two, scaled_two, inverse_two, gain[1])
            grad_attn = grad_hidden.astype(BF16)
            g_out_bias = jnp.sum(grad_attn.astype(F32), axis=0)
            grad_mixed = permute_columns(
                nt(grad_attn, in_out[:, 3 * width :]).astype(BF16), index, half, inverse=True
            )
            split = lambda v: v.reshape(rows, heads, HD)
            scores = jnp.einsum("qhe,khe->hqk", split(query), split(key), preferred_element_type=F32) * HD ** (-0.5)
            probs = jnp.exp(scores - log_total)
            grad_value = jnp.einsum("hqk,qhe->khe", probs.astype(BF16), split(grad_mixed), preferred_element_type=F32)
            grad_probs = jnp.einsum("qhe,khe->hqk", split(grad_mixed), split(value), preferred_element_type=F32)
            grad_scores = (
                probs * (grad_probs - jnp.sum(grad_probs * probs, axis=-1, keepdims=True))
            ).astype(BF16)
            grad_query = jnp.einsum("hqk,khe->qhe", grad_scores, split(key), preferred_element_type=F32) * HD ** (-0.5)
            grad_key = jnp.einsum("hqk,qhe->khe", grad_scores, split(query), preferred_element_type=F32) * HD ** (-0.5)
            grad_joint = jnp.concatenate(
                [item.reshape(rows, width) for item in (grad_query, grad_key, grad_value)], axis=1
            ).astype(BF16)
            sums = jnp.sum(grad_joint.astype(F32), axis=0)
            g_in_bias = jnp.concatenate([sums[:width], sums[2 * width :]])
            g_in_out = reduce_parts(
                lambda h, low, high: jnp.concatenate(
                    [
                        tn(columns(normed_one, h, low, high, half), grad_joint),
                        tn(columns(mixed, h, low, high, half), grad_attn),
                    ],
                    axis=1,
                ),
                half,
            )
            grad_normed_one = permute_columns(nt(grad_joint, in_out[:, : 3 * width]), index, half, inverse=True)
            gain_one = jnp.sum(grad_normed_one * scaled_one, axis=0)
            shift_one = jnp.sum(grad_normed_one, axis=0)
            grad_inputs = grad_hidden + norm_back(grad_normed_one, scaled_one, inverse_one, gain[0])
            g_small = [
                jnp.stack([gain_one, gain_two]), jnp.stack([shift_one, shift_two]),
                g_in_bias, g_out_bias, g_up_bias, g_down_bias,
            ]
            return grad_inputs, (g_in_out, g_up, g_down), g_small

        grad_middle, big_one, small_one = backward_layer(seed.astype(F32), 1)
        grad_source, big_zero, small_zero = backward_layer(grad_middle.astype(BF16).astype(F32), 0)

        def packed(items):
            parts = []
            for item in items:
                if item.ndim == 2:
                    parts.append(item.reshape(2, fsdp, -1).transpose(1, 0, 2).reshape(fsdp, -1))
                else:
                    parts.append(item.reshape(fsdp, -1))
            flat = jnp.concatenate(parts, axis=1)
            return jnp.pad(flat, ((0, 0), (0, -small_size % 1024))).reshape(fsdp, -1, 1024)

        both = jnp.concatenate([packed(small_zero), packed(small_one)], axis=1)
        relative = jnp.take(both, small_order, axis=0)
        flat_rows = both.shape[1]
        relative = relative.reshape(fsdp * flat_rows, 1024)
        turned = jnp.take(both, jnp.stack(
            [links.at ^ jnp.where(first, links.offset(1, j), links.offset(0, j)) for j in range(fsdp)]), axis=0
        ).reshape(fsdp * flat_rows, 1024)
        small_total = reduce_parts(
            lambda h, low, high: (turned if h else relative)[low * flat_rows : high * flat_rows], flat_rows
        ).astype(F32)
        small_total = jnp.where(first, small_total[:small_rows], small_total[small_rows:]).reshape(-1)[:small_size]

        outs = []
        for zero, one in zip(big_zero, big_one):
            moved = swap(jnp.where(first, one, zero))
            stay = jnp.where(first, zero, one)
            low = jnp.where(first, stay, moved)
            high = jnp.where(first, moved, stay)
            outs.append(jnp.concatenate([low, high], axis=0).astype(F32))
        g_in_out, g_up, g_down = outs

        crossed = swap(jnp.where(first, final, grad_source))
        in_order = jnp.stack(
            [jnp.where(assign[0, 0] == 0, grad_source, crossed), jnp.where(assign[0, 0] == 0, crossed, grad_source)]
        )
        ends = jnp.where(first, in_order, jnp.stack([crossed, final]))[None]

        at, pieces = 0, []
        for shape in ((2, part), (2, part), (2 * part,), (part,), (4 * part,), (part,)):
            count = 1
            for size in shape:
                count *= size
            pieces.append(small_total[at : at + count].reshape((1,) + shape))
            at += count
        gain, shift, in_bias, out_bias, up_bias, down_bias_grad = pieces
        return (
            ends, gain, shift, g_in_out[None, :, : 3 * width], in_bias, g_in_out[None, :, 3 * width :],
            out_bias, g_up[None], up_bias, g_down[None], down_bias_grad,
        )

    vector, matrix = P("section", "fsdp"), P("section", "fsdp", None)
    pair = P("section", None, "fsdp")
    rows = P(("fsdp", "replica"), None, None)
    return jax.shard_map(
        per_device,
        mesh=mesh,
        in_specs=(rows, P(("fsdp", "replica"), None), rows, pair, pair, matrix, vector, matrix, vector, matrix, vector, matrix, vector),
        out_specs=(
            P("section", ("fsdp", "replica"), None, None), pair, pair, matrix, vector, matrix, vector, matrix, vector, matrix, vector,
        ),
        check_vma=False,
    )
```
